32 devices in a mesh: vir: 8 (over z, y), fit: 4 (over x, core).
Axes of the slice: x: 2, y: 2, z: 4, core: 2. Of those that a mesh axis runs over, the one named last changes fastest.
Arguments:
- fitted: bfloat16 [2, 2400, 24, 7168], P(None, 'vir', None, 'fit'), may hold values from -0.0234375 to 0.0234375
- vcouple: bfloat16 [2, 2400, 2400], P(None, 'fit'), may hold values from -0.125 to 0.125
- actfock: float32 [2, 24, 24], replicated, may hold values from -1.25 to 1.25
- eps_vir: float32 [2400], P('vir'), may hold values from 0.5 to 4
- eps_act: float32 [24], replicated, may hold values from -0.5 to 0.5
- pair_energy: float32 [64], replicated, may hold values from -3 to -2
- source: float32 [2, 2400, 1536], P(None, 'vir'), may hold values from -6 to 6
Outputs:
- amplitude: float32 [2, 2400, 1536], P(None, 'vir')
The draws below stay inside these ranges and needn't reach their ends.
All inputs are finite; a program needn't handle non-finite values.
Results may differ from the reference program's by a relative error of at most 0.0026.
Values may be sent and summed in bfloat16 or wider, within the bound.
A program may use at most 256 MiB of HBM per device.

```python
import math
import jax
import jax.numpy as jnp
from jax import lax

NACT = 24
NVIR = 2400
NFIT = 7168
PAIRS = 64
PASSES = 3


def steps_of(rng, shape, split, low, top_value):
    factor_of = 1.0
    for position, blocks in split:
        draws = jax.random.uniform(jax.random.fold_in(jax.random.fold_in(rng, 6), position), (blocks,), jnp.float32, low / len(split), top_value / len(split))
        factor_of = factor_of * jnp.repeat(jnp.exp(draws), shape[position] // blocks).reshape((-1,) + (1,) * (len(shape) - 1 - position))
    return factor_of


def scatter_about(rng, shape, scale, bound, shards=(), kind=jnp.bfloat16):
    entries = scale * jax.random.normal(rng, shape, jnp.float32)
    if shards:
        entries = entries * steps_of(rng, shape, shards, -0.22, 0.18)
    return jnp.clip(entries, -bound, bound).astype(kind)


def setup_inputs(seed: int = 0) -> dict:
    arg_keys = jax.random.split(jax.random.key(seed), 8)
    fitted = scatter_about(arg_keys[0], (2, NVIR, NACT, NFIT), (NACT * NVIR) ** -0.5, 0.0234375, ((1, 8), (3, 4)))
    vcouple = scatter_about(arg_keys[1], (2, NVIR, NVIR), NVIR ** -0.5, 0.125, ((1, 4),))
    actfock = scatter_about(arg_keys[2], (2, NACT, NACT), NACT ** -0.5, 1.25, (), jnp.float32)
    eps_vir = jnp.clip(jnp.exp(math.log(4.0) - 2.0794415 * jax.random.uniform(arg_keys[3], (NVIR,), jnp.float32) ** steps_of(arg_keys[3], (NVIR,), ((0, 8),), -0.2, 0.2)), 0.5, 4.0)
    eps_act = jnp.clip(jax.random.uniform(arg_keys[4], (NACT,), jnp.float32, -0.5, 0.5), -0.5, 0.5)
    pair_energy = jnp.clip(jax.random.uniform(arg_keys[5], (PAIRS,), jnp.float32, -3.0, -2.0), -3.0, -2.0)
    source = scatter_about(arg_keys[6], (2, NVIR, NACT * PAIRS), 1.0, 6.0, ((1, 8),), jnp.float32)
    return {"fitted": fitted, "vcouple": vcouple, "actfock": actfock, "eps_vir": eps_vir, "eps_act": eps_act, "pair_energy": pair_energy, "source": source}


def product(left, right):
    return jnp.dot(left, right, precision=lax.Precision.HIGHEST, preferred_element_type=jnp.float32)


def product_first(left, right):
    return lax.dot_general(left, right, (((0,), (0,)), ((), ())), precision=lax.Precision.HIGHEST, preferred_element_type=jnp.float32)


def reference(fitted, vcouple, actfock, eps_vir, eps_act, pair_energy, source):
    highest = lax.Precision.HIGHEST
    denominator = (eps_vir[:, None, None] + eps_act[None, :, None] - pair_energy[None, None, :]).reshape(NVIR, NACT * PAIRS)
    amplitude = source / denominator[None]
    width = NVIR * NACT
    fit_block = NFIT // 8
    fit_real = fitted[0].reshape(width, NFIT)
    fit_imag = fitted[1].reshape(width, NFIT)
    couple_real = vcouple[0].astype(jnp.float32)
    couple_imag = vcouple[1].astype(jnp.float32)
    for pass_index in range(PASSES):
        rounded = amplitude.astype(jnp.bfloat16)
        flat_real = rounded[0].reshape(width, PAIRS).astype(jnp.float32)
        flat_imag = rounded[1].reshape(width, PAIRS).astype(jnp.float32)

        def block(carry, index):
            start = (index * fit_block).astype(jnp.int32)
            piece_real = lax.dynamic_slice_in_dim(fit_real, start, fit_block, 1).astype(jnp.float32)
            piece_imag = lax.dynamic_slice_in_dim(fit_imag, start, fit_block, 1).astype(jnp.float32)
            over_real = product_first(piece_real, flat_real) + product_first(piece_imag, flat_imag)
            over_imag = product_first(piece_real, flat_imag) - product_first(piece_imag, flat_real)
            over_real = lax.optimization_barrier(over_real.astype(jnp.bfloat16)).astype(jnp.float32)
            over_imag = lax.optimization_barrier(over_imag.astype(jnp.bfloat16)).astype(jnp.float32)
            sum_real = carry[0] + product(piece_real, over_real) - product(piece_imag, over_imag)
            sum_imag = carry[1] + product(piece_real, over_imag) + product(piece_imag, over_real)
            return (sum_real, sum_imag), None

        zeros = jnp.zeros((width, PAIRS), jnp.float32)
        sums, ignored = lax.scan(block, (zeros, zeros), jnp.arange(8, dtype=jnp.int32))
        fitted_term = jnp.stack([sums[0], sums[1]]).reshape(2, NVIR, NACT * PAIRS)
        rows_real = rounded[0].astype(jnp.float32)
        rows_imag = rounded[1].astype(jnp.float32)
        vir_real = product_first(couple_real, rows_real) - product_first(couple_imag, rows_imag)
        vir_imag = product_first(couple_imag, rows_real) + product_first(couple_real, rows_imag)
        virtual_term = jnp.stack([vir_real, vir_imag])
        values = amplitude.reshape(2, NVIR, NACT, PAIRS)
        act_real = jnp.einsum("aup,ut->atp", values[0], actfock[0], precision=highest) - jnp.einsum("aup,ut->atp", values[1], actfock[1], precision=highest)
        act_imag = jnp.einsum("aup,ut->atp", values[0], actfock[1], precision=highest) + jnp.einsum("aup,ut->atp", values[1], actfock[0], precision=highest)
        active_term = jnp.stack([act_real, act_imag]).reshape(2, NVIR, NACT * PAIRS)
        residual = source - denominator[None] * amplitude - active_term - fitted_term - virtual_term
        amplitude = amplitude + residual / denominator[None]
    return amplitude
```

```python
import jax
import jax.numpy as jnp
from jax import lax
from jax.experimental import pallas as pl
from jax.experimental.pallas import tpu as pltpu
from jax.sharding import PartitionSpec as P

PASSES = 3


def contract_first(left, right):
    return lax.dot_general(
        left, right, (((0,), (0,)), ((), ())), preferred_element_type=jnp.float32
    )


def plain_product(left, right):
    return jnp.dot(left, right, preferred_element_type=jnp.float32)


def active_coupling(values, actfock, active, pairs):
    highest = lax.Precision.HIGHEST
    local_vir = values.shape[1]
    grid = values.reshape(2, local_vir, active, pairs)
    act_real = jnp.einsum("aup,ut->atp", grid[0], actfock[0], precision=highest) - jnp.einsum(
        "aup,ut->atp", grid[1], actfock[1], precision=highest
    )
    act_imag = jnp.einsum("aup,ut->atp", grid[0], actfock[1], precision=highest) + jnp.einsum(
        "aup,ut->atp", grid[1], actfock[0], precision=highest
    )
    return jnp.stack([act_real, act_imag]).reshape(2, local_vir, actfock.shape[2] * pairs)


def plain_device(fitted, vcouple, actfock, eps_vir, eps_act, pair_energy, source):
    local_vir = fitted.shape[1]
    active = fitted.shape[2]
    local_fit = fitted.shape[3]
    pairs = pair_energy.shape[0]
    block_rows = vcouple.shape[1]
    width = local_vir * active
    fit_index = lax.axis_index("fit")
    denominator = (
        eps_vir[:, None, None] + eps_act[None, :, None] - pair_energy[None, None, :]
    ).reshape(local_vir, active * pairs)
    amplitude = source / denominator[None]
    fit_real = fitted[0].reshape(width, local_fit)
    fit_imag = fitted[1].reshape(width, local_fit)
    for pass_index in range(PASSES):
        rounded = amplitude.astype(jnp.bfloat16)
        flat_both = jnp.concatenate(
            [rounded[0].reshape(width, pairs), rounded[1].reshape(width, pairs)], axis=1
        )
        real_side = contract_first(fit_real, flat_both)
        imag_side = contract_first(fit_imag, flat_both)
        over_real = real_side[:, :pairs] + imag_side[:, pairs:]
        over_imag = real_side[:, pairs:] - imag_side[:, :pairs]
        intersection = lax.psum(jnp.concatenate([over_real, over_imag], axis=1), "vir").astype(
            jnp.bfloat16
        )
        real_out = plain_product(fit_real, intersection)
        imag_out = plain_product(fit_imag, intersection)
        sum_real = real_out[:, :pairs] - imag_out[:, pairs:]
        sum_imag = real_out[:, pairs:] + imag_out[:, :pairs]
        fitted_part = jnp.stack([sum_real, sum_imag]).reshape(2, local_vir, active * pairs)
        regrouped = lax.all_to_all(rounded, "vir", split_axis=2, concat_axis=1, tiled=True)
        window = lax.dynamic_slice_in_dim(regrouped, fit_index * block_rows, block_rows, 1)
        couple_real = contract_first(vcouple[0], window[0]) - contract_first(vcouple[1], window[1])
        couple_imag = contract_first(vcouple[1], window[0]) + contract_first(vcouple[0], window[1])
        coupled = jnp.stack([couple_real, couple_imag])
        returned = lax.all_to_all(coupled, "vir", split_axis=1, concat_axis=2, tiled=True)
        fitted_part = fitted_part + returned
        total = lax.psum(fitted_part, "fit")
        part_amplitude = amplitude
        active_term = active_coupling(amplitude, actfock, active, pairs)
        residual = source - denominator[None] * part_amplitude - active_term - total
        updated = part_amplitude + residual / denominator[None]
        amplitude = updated
    return amplitude


ROW_CHUNKS = 3
ROW_TILE = 512
VIR_TILE = 16


def turn(values, pairs):
    return jnp.concatenate([-values[..., pairs:], values[..., :pairs]], axis=-1)


def swap(values, bit):
    size = lax.axis_size("fit")
    return lax.ppermute(values, "fit", [(i, i ^ bit) for i in range(size)])


def pick(values, index, axis):
    return lax.dynamic_index_in_dim(values, index, axis, keepdims=False)


def fit_reduce(values, index):
    size = lax.axis_size("fit")
    stage = 1
    values = values.reshape(size, -1, values.shape[-1])
    while stage < size:
        left = values.shape[0]
        grid = values.reshape(left // 2, 2, *values.shape[1:])
        side = (index // stage) % 2
        sent = pick(grid, 1 - side, 1).astype(jnp.bfloat16)
        values = pick(grid, side, 1) + swap(sent, stage).astype(jnp.float32)
        stage *= 2
    return values[0]


def fit_gather(values, index):
    size = lax.axis_size("fit")
    stage = size // 2
    values = values[None]
    while stage >= 1:
        other = swap(values, stage)
        side = (index // stage) % 2
        first = jnp.where(side == 0, values, other)
        second = jnp.where(side == 0, other, values)
        values = jnp.stack([first, second], axis=1).reshape(-1, *values.shape[1:])
        stage //= 2
    return values.reshape(-1, values.shape[-1])


def vir_sum(values):
    size = lax.axis_size("vir")
    rows, lanes = values.shape
    parts = lax.all_to_all(
        values.astype(jnp.bfloat16).reshape(size, rows // size, lanes), "vir", 0, 0
    )
    own = jnp.sum(parts.astype(jnp.float32), axis=0).astype(jnp.bfloat16)
    spread = jnp.broadcast_to(own[None], (size, rows // size, lanes))
    return lax.all_to_all(spread, "vir", 0, 0).reshape(rows, lanes)


def back_kernel(fit_ref, inter_ref, turned_ref, virtual_ref, out_ref):
    out_ref[...] = (
        plain_product(fit_ref[0], inter_ref[...])
        + plain_product(fit_ref[1], turned_ref[...])
        + virtual_ref[...]
    )


def tile_of(rows):
    return max(t for t in range(16, ROW_TILE + 1, 16) if rows % t == 0)


def back_product(fit_rows, inter, turned, virtual, first, rows):
    depth, lanes = inter.shape
    tile = tile_of(rows)
    skip = first // tile
    return pl.pallas_call(
        back_kernel,
        grid=(rows // tile,),
        in_specs=[
            pl.BlockSpec((2, tile, depth), lambda i: (0, i + skip, 0)),
            pl.BlockSpec((depth, lanes), lambda i: (0, 0)),
            pl.BlockSpec((depth, lanes), lambda i: (0, 0)),
            pl.BlockSpec((tile, lanes), lambda i: (i + skip, 0)),
        ],
        out_specs=pl.BlockSpec((tile, lanes), lambda i: (i, 0)),
        out_shape=jax.ShapeDtypeStruct((rows, lanes), jnp.float32),
        cost_estimate=pl.CostEstimate(
            flops=4 * rows * depth * lanes,
            bytes_accessed=4 * rows * depth + 8 * rows * lanes,
            transcendentals=0,
        ),
        compiler_params=pltpu.CompilerParams(vmem_limit_bytes=24 * 2**20),
    )(fit_rows, inter, turned, virtual)


def virtual_kernel(pairs, couple_ref, rows_ref, out_ref):
    lanes = 2 * pairs
    for t in range(out_ref.shape[1]):
        block = rows_ref[:, t * lanes : (t + 1) * lanes]
        out_ref[:, t, :] = plain_product(couple_ref[0], block) + plain_product(
            couple_ref[1], turn(block, pairs)
        )


def virtual_product(couple, rows, active, pairs):
    lanes = 2 * pairs
    out, depth = couple.shape[1:]
    group = 8
    return pl.pallas_call(
        lambda *refs: virtual_kernel(pairs, *refs),
        grid=(active // group,),
        in_specs=[
            pl.BlockSpec((2, out, depth), lambda i: (0, 0, 0)),
            pl.BlockSpec((depth, group * lanes), lambda i: (0, i)),
        ],
        out_specs=pl.BlockSpec((out, group, lanes), lambda i: (0, i, 0)),
        out_shape=jax.ShapeDtypeStruct((out, active, lanes), jnp.float32),
        cost_estimate=pl.CostEstimate(
            flops=4 * out * depth * active * lanes,
            bytes_accessed=2 * depth * active * lanes + 4 * out * active * lanes,
            transcendentals=0,
        ),
        compiler_params=pltpu.CompilerParams(vmem_limit_bytes=24 * 2**20),
    )(couple, rows)


def per_device(fitted, vcouple, actfock, eps_vir, eps_act, pair_energy, source):
    n_fit, n_vir = lax.axis_size("fit"), lax.axis_size("vir")
    fit_index, vir_index = lax.axis_index("fit"), lax.axis_index("vir")
    local_vir, active, local_fit = fitted.shape[1:]
    pairs = pair_energy.shape[0]
    lanes = 2 * pairs
    spread = n_vir // n_fit
    chunk_vir = local_vir // ROW_CHUNKS
    own_vir = chunk_vir // n_fit
    chunk_rows = chunk_vir * active
    highest = lax.Precision.HIGHEST

    denominator = eps_vir[:, None, None] + eps_act[None, :, None] - pair_energy[None, None, :]
    denominator = jnp.concatenate([denominator, denominator], axis=2)
    grid = source.reshape(2, local_vir, active, pairs)
    joined = jnp.concatenate([grid[0], grid[1]], axis=2)
    start = joined / denominator

    def own(values, chunk):
        return lax.dynamic_slice_in_dim(
            values, chunk * chunk_vir + fit_index * own_vir, own_vir, 0
        )

    own_source = [own(joined, c) for c in range(ROW_CHUNKS)]
    own_denominator = [own(denominator, c) for c in range(ROW_CHUNKS)]
    own_start = [own(start, c) for c in range(ROW_CHUNKS)]
    amplitude = own_start
    fit_rows = fitted.reshape(2, local_vir * active, local_fit)
    own_rows = ROW_CHUNKS * own_vir
    padded = -(-own_rows // VIR_TILE) * VIR_TILE
    couple = lax.dynamic_slice_in_dim(vcouple, vir_index * local_vir, local_vir, 2)
    couple = couple.reshape(2, spread, ROW_CHUNKS, n_fit, own_vir, local_vir)
    couple = couple.transpose(0, 5, 1, 3, 2, 4).reshape(2, local_vir, n_vir, own_rows)
    couple = jnp.pad(couple, ((0, 0), (0, 0), (0, 0), (0, padded - own_rows)))
    couple = couple.reshape(2, local_vir, n_vir * padded)
    gathered = [
        start[c * chunk_vir : (c + 1) * chunk_vir].reshape(chunk_rows, lanes).astype(jnp.bfloat16)
        for c in range(ROW_CHUNKS)
    ]
    own_rounded = [a.astype(jnp.bfloat16) for a in amplitude]
    route = [
        (u * n_fit + g, ((u % spread) * n_fit + g) * n_fit + u // spread)
        for u in range(n_vir)
        for g in range(n_fit)
    ]
    fit_whole = fitted.reshape(2 * local_vir * active, local_fit)
    for pass_index in range(PASSES):
        mine = jnp.concatenate(own_rounded).reshape(own_rows, active * lanes)
        mine = jnp.pad(mine, ((0, padded - own_rows), (0, 0)))
        moved = lax.ppermute(mine, ("vir", "fit"), route)
        rows = lax.all_gather(moved, "vir", axis=0, tiled=True)
        virtual = virtual_product(couple, rows, active, pairs)
        virtual = virtual.reshape(local_vir * active, lanes)

        both = jnp.concatenate(gathered + [-turn(g, pairs) for g in gathered])
        inter = vir_sum(contract_first(fit_whole, both))
        inter_turned = turn(inter, pairs)
        last = pass_index == PASSES - 1
        updated = []
        gathered = []
        for c in range(ROW_CHUNKS):
            term = back_product(
                fit_rows, inter, inter_turned, virtual, c * chunk_rows, chunk_rows
            )
            total = fit_reduce(term, fit_index).reshape(own_vir, active, lanes)
            value = amplitude[c]
            act = jnp.einsum("aul,ut->atl", value, actfock[0], precision=highest) + jnp.einsum(
                "aul,ut->atl", turn(value, pairs), actfock[1], precision=highest
            )
            residual = own_source[c] - own_denominator[c] * value - act - total
            value = value + residual / own_denominator[c]
            updated.append(value)
            sent = value - own_start[c] if last else value
            gathered.append(
                fit_gather(sent.reshape(-1, lanes).astype(jnp.bfloat16), fit_index)
            )
        amplitude = updated
        own_rounded = [a.astype(jnp.bfloat16) for a in amplitude]
    change = jnp.concatenate(gathered).reshape(local_vir, active, lanes).astype(jnp.float32)
    result = start + change
    return jnp.stack([result[..., :pairs], result[..., pairs:]]).reshape(source.shape)


def choose(mesh):
    def body(*args):
        n_fit, n_vir = mesh.shape["fit"], mesh.shape["vir"]
        fitted = args[0]
        fits = (
            n_vir % n_fit == 0
            and n_fit & (n_fit - 1) == 0
            and fitted.shape[1] % (ROW_CHUNKS * n_fit) == 0
            and fitted.shape[2] % 8 == 0
            and fitted.shape[3] % (16 * n_vir) == 0
            and fitted.shape[1] * fitted.shape[2] % (16 * ROW_CHUNKS) == 0
        )
        return per_device(*args) if fits else plain_device(*args)

    return body


def solution(mesh):
    return jax.shard_map(
        choose(mesh),
        mesh=mesh,
        in_specs=(
            P(None, "vir", None, "fit"),
            P(None, "fit", None),
            P(),
            P("vir"),
            P(),
            P(),
            P(None, "vir", None),
        ),
        out_specs=P(None, "vir", None),
        check_vma=False,
    )
```

```python
import jax
import jax.numpy as jnp
from jax import lax
from jax.experimental import pallas as pl
from jax.experimental.pallas import tpu as pltpu
from jax.sharding import PartitionSpec as P

PASSES = 3


def contract_first(left, right):
    return lax.dot_general(
        left, right, (((0,), (0,)), ((), ())), preferred_element_type=jnp.float32
    )


def plain_product(left, right):
    return jnp.dot(left, right, preferred_element_type=jnp.float32)


def active_coupling(values, actfock, active, pairs):
    highest = lax.Precision.HIGHEST
    local_vir = values.shape[1]
    grid = values.reshape(2, local_vir, active, pairs)
    act_real = jnp.einsum("aup,ut->atp", grid[0], actfock[0], precision=highest) - jnp.einsum(
        "aup,ut->atp", grid[1], actfock[1], precision=highest
    )
    act_imag = jnp.einsum("aup,ut->atp", grid[0], actfock[1], precision=highest) + jnp.einsum(
        "aup,ut->atp", grid[1], actfock[0], precision=highest
    )
    return jnp.stack([act_real, act_imag]).reshape(2, local_vir, actfock.shape[2] * pairs)


def plain_device(fitted, vcouple, actfock, eps_vir, eps_act, pair_energy, source):
    local_vir = fitted.shape[1]
    active = fitted.shape[2]
    local_fit = fitted.shape[3]
    pairs = pair_energy.shape[0]
    block_rows = vcouple.shape[1]
    width = local_vir * active
    fit_index = lax.axis_index("fit")
    denominator = (
        eps_vir[:, None, None] + eps_act[None, :, None] - pair_energy[None, None, :]
    ).reshape(local_vir, active * pairs)
    amplitude = source / denominator[None]
    fit_real = fitted[0].reshape(width, local_fit)
    fit_imag = fitted[1].reshape(width, local_fit)
    for pass_index in range(PASSES):
        rounded = amplitude.astype(jnp.bfloat16)
        flat_both = jnp.concatenate(
            [rounded[0].reshape(width, pairs), rounded[1].reshape(width, pairs)], axis=1
        )
        real_side = contract_first(fit_real, flat_both)
        imag_side = contract_first(fit_imag, flat_both)
        over_real = real_side[:, :pairs] + imag_side[:, pairs:]
        over_imag = real_side[:, pairs:] - imag_side[:, :pairs]
        intersection = lax.psum(jnp.concatenate([over_real, over_imag], axis=1), "vir").astype(
            jnp.bfloat16
        )
        real_out = plain_product(fit_real, intersection)
        imag_out = plain_product(fit_imag, intersection)
        sum_real = real_out[:, :pairs] - imag_out[:, pairs:]
        sum_imag = real_out[:, pairs:] + imag_out[:, :pairs]
        fitted_part = jnp.stack([sum_real, sum_imag]).reshape(2, local_vir, active * pairs)
        regrouped = lax.all_to_all(rounded, "vir", split_axis=2, concat_axis=1, tiled=True)
        window = lax.dynamic_slice_in_dim(regrouped, fit_index * block_rows, block_rows, 1)
        couple_real = contract_first(vcouple[0], window[0]) - contract_first(vcouple[1], window[1])
        couple_imag = contract_first(vcouple[1], window[0]) + contract_first(vcouple[0], window[1])
        coupled = jnp.stack([couple_real, couple_imag])
        returned = lax.all_to_all(coupled, "vir", split_axis=1, concat_axis=2, tiled=True)
        fitted_part = fitted_part + returned
        total = lax.psum(fitted_part, "fit")
        part_amplitude = amplitude
        active_term = active_coupling(amplitude, actfock, active, pairs)
        residual = source - denominator[None] * part_amplitude - active_term - total
        updated = part_amplitude + residual / denominator[None]
        amplitude = updated
    return amplitude


ROW_CHUNKS = 1
ROW_TILE = 512
VIR_TILE = 16


def turn(values, pairs):
    return jnp.concatenate([-values[..., pairs:], values[..., :pairs]], axis=-1)


def swap(values, bit):
    size = lax.axis_size("fit")
    return lax.ppermute(values, "fit", [(i, i ^ bit) for i in range(size)])


def pick(values, index, axis):
    return lax.dynamic_index_in_dim(values, index, axis, keepdims=False)


def fit_reduce(values, index):
    size = lax.axis_size("fit")
    stage = 1
    values = values.reshape(size, -1, values.shape[-1])
    while stage < size:
        left = values.shape[0]
        grid = values.reshape(left // 2, 2, *values.shape[1:])
        side = (index // stage) % 2
        sent = pick(grid, 1 - side, 1).astype(jnp.bfloat16)
        values = pick(grid, side, 1) + swap(sent, stage).astype(jnp.float32)
        stage *= 2
    return values[0]


def fit_gather(values, index):
    size = lax.axis_size("fit")
    stage = size // 2
    values = values[None]
    while stage >= 1:
        other = swap(values, stage)
        side = (index // stage) % 2
        first = jnp.where(side == 0, values, other)
        second = jnp.where(side == 0, other, values)
        values = jnp.stack([first, second], axis=1).reshape(-1, *values.shape[1:])
        stage //= 2
    return values.reshape(-1, values.shape[-1])


def vir_sum(values):
    size = lax.axis_size("vir")
    rows, lanes = values.shape
    parts = lax.all_to_all(
        values.astype(jnp.bfloat16).reshape(size, rows // size, lanes), "vir", 0, 0
    )
    own = jnp.sum(parts.astype(jnp.float32), axis=0).astype(jnp.bfloat16)
    spread = jnp.broadcast_to(own[None], (size, rows // size, lanes))
    return lax.all_to_all(spread, "vir", 0, 0).reshape(rows, lanes)


def back_kernel(fit_ref, inter_ref, turned_ref, virtual_ref, out_ref):
    out_ref[...] = (
        plain_product(fit_ref[0], inter_ref[...])
        + plain_product(fit_ref[1], turned_ref[...])
        + virtual_ref[...]
    )


def tile_of(rows):
    return max(t for t in range(16, ROW_TILE + 1, 16) if rows % t == 0)


def back_product(fit_rows, inter, turned, virtual, first, rows):
    depth, lanes = inter.shape
    tile = tile_of(rows)
    skip = first // tile
    return pl.pallas_call(
        back_kernel,
        grid=(rows // tile,),
        in_specs=[
            pl.BlockSpec((2, tile, depth), lambda i: (0, i + skip, 0)),
            pl.BlockSpec((depth, lanes), lambda i: (0, 0)),
            pl.BlockSpec((depth, lanes), lambda i: (0, 0)),
            pl.BlockSpec((tile, lanes), lambda i: (i + skip, 0)),
        ],
        out_specs=pl.BlockSpec((tile, lanes), lambda i: (i, 0)),
        out_shape=jax.ShapeDtypeStruct((rows, lanes), jnp.float32),
        cost_estimate=pl.CostEstimate(
            flops=4 * rows * depth * lanes,
            bytes_accessed=4 * rows * depth + 8 * rows * lanes,
            transcendentals=0,
        ),
        compiler_params=pltpu.CompilerParams(vmem_limit_bytes=24 * 2**20),
    )(fit_rows, inter, turned, virtual)


def virtual_kernel(pairs, couple_ref, rows_ref, out_ref):
    lanes = 2 * pairs
    for t in range(out_ref.shape[1]):
        block = rows_ref[:, t * lanes : (t + 1) * lanes]
        out_ref[:, t, :] = plain_product(couple_ref[0], block) + plain_product(
            couple_ref[1], turn(block, pairs)
        )


def virtual_product(couple, rows, active, pairs):
    lanes = 2 * pairs
    out, depth = couple.shape[1:]
    group = 8
    return pl.pallas_call(
        lambda *refs: virtual_kernel(pairs, *refs),
        grid=(active // group,),
        in_specs=[
            pl.BlockSpec((2, out, depth), lambda i: (0, 0, 0)),
            pl.BlockSpec((depth, group * lanes), lambda i: (0, i)),
        ],
        out_specs=pl.BlockSpec((out, group, lanes), lambda i: (0, i, 0)),
        out_shape=jax.ShapeDtypeStruct((out, active, lanes), jnp.float32),
        cost_estimate=pl.CostEstimate(
            flops=4 * out * depth * active * lanes,
            bytes_accessed=2 * depth * active * lanes + 4 * out * active * lanes,
            transcendentals=0,
        ),
        compiler_params=pltpu.CompilerParams(vmem_limit_bytes=24 * 2**20),
    )(couple, rows)


def per_device(fitted, vcouple, actfock, eps_vir, eps_act, pair_energy, source):
    n_fit, n_vir = lax.axis_size("fit"), lax.axis_size("vir")
    fit_index, vir_index = lax.axis_index("fit"), lax.axis_index("vir")
    local_vir, active, local_fit = fitted.shape[1:]
    pairs = pair_energy.shape[0]
    lanes = 2 * pairs
    spread = n_vir // n_fit
    chunk_vir = local_vir // ROW_CHUNKS
    own_vir = chunk_vir // n_fit
    chunk_rows = chunk_vir * active
    highest = lax.Precision.HIGHEST

    denominator = eps_vir[:, None, None] + eps_act[None, :, None] - pair_energy[None, None, :]
    denominator = jnp.concatenate([denominator, denominator], axis=2)
    grid = source.reshape(2, local_vir, active, pairs)
    joined = jnp.concatenate([grid[0], grid[1]], axis=2)
    start = joined / denominator

    def own(values, chunk):
        return lax.dynamic_slice_in_dim(
            values, chunk * chunk_vir + fit_index * own_vir, own_vir, 0
        )

    own_source = [own(joined, c) for c in range(ROW_CHUNKS)]
    own_denominator = [own(denominator, c) for c in range(ROW_CHUNKS)]
    own_start = [own(start, c) for c in range(ROW_CHUNKS)]
    amplitude = own_start
    fit_rows = fitted.reshape(2, local_vir * active, local_fit)
    own_rows = ROW_CHUNKS * own_vir
    padded = -(-own_rows // VIR_TILE) * VIR_TILE
    couple = lax.dynamic_slice_in_dim(vcouple, vir_index * local_vir, local_vir, 2)
    couple = couple.reshape(2, spread, ROW_CHUNKS, n_fit, own_vir, local_vir)
    couple = couple.transpose(0, 5, 1, 3, 2, 4).reshape(2, local_vir, n_vir, own_rows)
    couple = jnp.pad(couple, ((0, 0), (0, 0), (0, 0), (0, padded - own_rows)))
    couple = couple.reshape(2, local_vir, n_vir * padded)
    gathered = [
        start[c * chunk_vir : (c + 1) * chunk_vir].reshape(chunk_rows, lanes).astype(jnp.bfloat16)
        for c in range(ROW_CHUNKS)
    ]
    own_rounded = [a.astype(jnp.bfloat16) for a in amplitude]
    route = [
        (u * n_fit + g, ((u % spread) * n_fit + g) * n_fit + u // spread)
        for u in range(n_vir)
        for g in range(n_fit)
    ]
    fit_whole = fitted.reshape(2 * local_vir * active, local_fit)
    for pass_index in range(PASSES):
        mine = jnp.concatenate(own_rounded).reshape(own_rows, active * lanes)
        mine = jnp.pad(mine, ((0, padded - own_rows), (0, 0)))
        moved = lax.ppermute(mine, ("vir", "fit"), route)
        rows = lax.all_gather(moved, "vir", axis=0, tiled=True)
        virtual = virtual_product(couple, rows, active, pairs)
        virtual = virtual.reshape(local_vir * active, lanes)

        both = jnp.concatenate(gathered + [-turn(g, pairs) for g in gathered])
        inter = vir_sum(contract_first(fit_whole, both))
        inter_turned = turn(inter, pairs)
        last = pass_index == PASSES - 1
        updated = []
        gathered = []
        for c in range(ROW_CHUNKS):
            term = back_product(
                fit_rows, inter, inter_turned, virtual, c * chunk_rows, chunk_rows
            )
            total = fit_reduce(term, fit_index).reshape(own_vir, active, lanes)
            value = amplitude[c]
            act = jnp.einsum("aul,ut->atl", value, actfock[0], precision=highest) + jnp.einsum(
                "aul,ut->atl", turn(value, pairs), actfock[1], precision=highest
            )
            residual = own_source[c] - own_denominator[c] * value - act - total
            value = value + residual / own_denominator[c]
            updated.append(value)
            sent = value - own_start[c] if last else value
            gathered.append(
                fit_gather(sent.reshape(-1, lanes).astype(jnp.bfloat16), fit_index)
            )
        amplitude = updated
        own_rounded = [a.astype(jnp.bfloat16) for a in amplitude]
        if not last:
            gathered, own_rounded = lax.optimization_barrier((gathered, own_rounded))
    change = jnp.concatenate(gathered).reshape(local_vir, active, lanes).astype(jnp.float32)
    result = start + change
    return jnp.stack([result[..., :pairs], result[..., pairs:]]).reshape(source.shape)


def choose(mesh):
    def body(*args):
        n_fit, n_vir = mesh.shape["fit"], mesh.shape["vir"]
        fitted = args[0]
        fits = (
            n_vir % n_fit == 0
            and n_fit & (n_fit - 1) == 0
            and fitted.shape[1] % (ROW_CHUNKS * n_fit) == 0
            and fitted.shape[2] % 8 == 0
            and fitted.shape[3] % (16 * n_vir) == 0
            and fitted.shape[1] * fitted.shape[2] % (16 * ROW_CHUNKS) == 0
        )
        return per_device(*args) if fits else plain_device(*args)

    return body


def solution(mesh):
    return jax.shard_map(
        choose(mesh),
        mesh=mesh,
        in_specs=(
            P(None, "vir", None, "fit"),
            P(None, "fit", None),
            P(),
            P("vir"),
            P(),
            P(),
            P(None, "vir", None),
        ),
        out_specs=P(None, "vir", None),
        check_vma=False,
    )
```
